32 devices in a mesh: seq: 4 (over y, x), head: 8 (over z, core).
Axes of the slice: x: 2, y: 2, z: 4, core: 2. Of those that a mesh axis runs over, the one named last changes fastest.
Arguments:
- sequence_activity: bfloat16 [2, 2048, 4096], P(None, 'seq', 'head'), may hold values from -6 to 6
- lookup_mapping_tensor: bfloat16 [4096, 8, 768], P(None, 'head'), may hold values from -1 to 1, as said below
- stepsize_mapping_matrix: bfloat16 [4096, 8], P(None, 'head'), may hold values from -0.09375 to 0.09375
- logit_sharpness: float32 [8], P('head'), may hold values from 4 to 120
- adapter_gain_vector: float32 [8, 256], P('head'), may hold values from 0.1 to 1.9
- starting_inner_left_matrix: float32 [8, 256, 512], P('head'), may hold values from -0.375 to 0.375
- starting_inner_right_matrix: float32 [8, 512, 256], P('head'), may hold values from -0.25 to 0.25
- final_mixing_matrix: bfloat16 [8, 256, 4096], P('head'), may hold values from -0.125 to 0.125
Outputs:
- mixed: bfloat16 [2, 2048, 4096], P(None, 'seq', 'head')
The draws below stay inside these ranges and needn't reach their ends.
Inputs may be any that keep to these rules, and one draw needn't show every extreme that they name: `lookup_mapping_tensor`: entries of order 1 / sqrt(4096).
All inputs are finite; a program needn't handle non-finite values.
Results may differ from the reference program's by a relative error of at most 0.02.
Values may be sent and summed in bfloat16 or wider, within the bound.
No kernel may reach another device: no remote copies, remote signals or barrier semaphores. Data moves between devices by JAX's collectives and lax.ppermute only.
A program may use at most 64 MiB of HBM per device.

```python
import math
import jax
import jax.numpy as jnp
from jax import lax

D = 4096
DH = 256
HID = 512
GROUP = 512
WIN = 2048
NS_STEPS = 3
SEQS = 2
HEADS = 8
L = 2048
N_SEQ = 4


def draw_lookup_mapping_tensor(key, part):
    base = jax.random.truncated_normal(key, -6.0, 6.0, (D, HEADS, 3 * DH), jnp.float32)
    return (base / math.sqrt(D)).astype(jnp.bfloat16)


def draw_logit_sharpness(key, part):
    uniform_part = jax.random.uniform(key, (HEADS,), jnp.float32)
    lower, upper = (4.0, 24.0)
    return jnp.exp(math.log(lower) + uniform_part * (math.log(upper) - math.log(lower))).astype(jnp.float32)


def steps_of(key, extent, cuts, low, top_value):
    factor_of, own = 1.0, jax.random.fold_in(key, 6)
    for dim, parts in cuts:
        steps = jnp.exp(jax.random.uniform(jax.random.fold_in(own, dim), (parts,), jnp.float32, low / len(cuts), top_value / len(cuts)))
        factor_of = factor_of * jnp.repeat(steps, extent[dim] // parts).reshape([-1 if axis == dim else 1 for axis in range(len(extent))])
    return factor_of


def centred(key, shape, scale, most, cuts=(), kind=jnp.bfloat16):
    level = steps_of(key, shape, cuts, -0.22, 0.18) if cuts else 1.0
    result = jax.random.normal(key, shape, jnp.float32) * scale * level
    return jnp.minimum(jnp.maximum(result, -most), most).astype(kind)


def setup_inputs(seed: int = 0) -> dict:
    key_of = jax.random.split(jax.random.key(seed), 9)
    return {
        "sequence_activity": centred(key_of[0], (SEQS, L, D), 1.0, 6.0, ((1, 4), (2, 8))),
        "lookup_mapping_tensor": draw_lookup_mapping_tensor(jax.random.fold_in(key_of[8], 71), 0),
        "stepsize_mapping_matrix": centred(key_of[2], (D, HEADS), D ** -0.5, 0.09375, ((1, 8),)),
        "logit_sharpness": draw_logit_sharpness(jax.random.fold_in(key_of[8], 71), 0),
        "adapter_gain_vector": jnp.clip(1.0 + 0.18 * jax.random.normal(key_of[4], (HEADS, DH), jnp.float32), 0.1, 1.9),
        "starting_inner_left_matrix": centred(key_of[5], (HEADS, DH, HID), DH ** -0.5, 0.375, ((0, 8),), jnp.float32),
        "starting_inner_right_matrix": centred(key_of[6], (HEADS, HID, DH), HID ** -0.5, 0.25, ((0, 8),), jnp.float32),
        "final_mixing_matrix": centred(key_of[7], (HEADS, DH, D), (HEADS * DH) ** -0.5, 0.125, ((0, 8),)),
    }


update_rate = 0.3

def orthogonalize(update):
    scale = lax.rsqrt(jnp.sum(update * update) + 1e-06)
    current = update * scale
    for sweep in range(NS_STEPS):
        if current.shape[0] <= current.shape[1]:
            gram = jnp.dot(current, current.T, precision=lax.Precision.HIGHEST)
            current = 1.5 * current - 0.5 * jnp.dot(gram, current, precision=lax.Precision.HIGHEST)
        else:
            gram = jnp.dot(current.T, current, precision=lax.Precision.HIGHEST)
            current = 1.5 * current - 0.5 * jnp.dot(current, gram, precision=lax.Precision.HIGHEST)
    return current

def fast_group(weight_in, weight_out, keys, weighted, query_rows):
    in_half = weight_in.astype(jnp.bfloat16)
    out_half = weight_out.astype(jnp.bfloat16)
    hidden = jnp.dot(keys, in_half, preferred_element_type=jnp.float32)
    gating = jax.nn.sigmoid(hidden)
    activated = (hidden * gating).astype(jnp.bfloat16)
    grad_out = jnp.dot(activated.T, weighted, preferred_element_type=jnp.float32)
    backward = jnp.dot(weighted, out_half.T, preferred_element_type=jnp.float32)
    slopes = (backward * gating * (1.0 + hidden * (1.0 - gating))).astype(jnp.bfloat16)
    grad_in = jnp.dot(keys.T, slopes, preferred_element_type=jnp.float32)
    new_in = weight_in + update_rate * orthogonalize(grad_in)
    new_out = weight_out + update_rate * orthogonalize(grad_out)
    query_hidden = jnp.dot(query_rows, new_in.astype(jnp.bfloat16), preferred_element_type=jnp.float32)
    query_act = jax.nn.silu(query_hidden).astype(jnp.bfloat16)
    fast = jnp.dot(query_act, new_out.astype(jnp.bfloat16), preferred_element_type=jnp.float32)
    return (new_in, new_out, fast)

def prepare(projected, rate_col, count_seqs):
    head_dim = projected.shape[1] // 3
    query_rows = projected[:, :head_dim]
    keys = projected[:, head_dim:2 * head_dim]
    values = projected[:, 2 * head_dim:]
    query_norm = (query_rows * lax.rsqrt(lax.optimization_barrier(jnp.sum(query_rows * query_rows, axis=1, keepdims=True)) + 1e-06)).astype(jnp.bfloat16)
    key_norm = (keys * lax.rsqrt(lax.optimization_barrier(jnp.sum(keys * keys, axis=1, keepdims=True)) + 1e-06)).astype(jnp.bfloat16)
    value_half = values.astype(jnp.bfloat16)
    weighted = (jax.nn.softplus(rate_col) * values).astype(jnp.bfloat16)
    return (query_norm.reshape(count_seqs, -1, head_dim), key_norm.reshape(count_seqs, -1, head_dim), value_half.reshape(count_seqs, -1, head_dim), weighted.reshape(count_seqs, -1, head_dim))

def attend_window(query_rows, keys, values, scale, start):
    count = query_rows.shape[1]
    window = keys.shape[1] - count
    scores = scale * jnp.einsum('sqd,skd->sqk', query_rows.astype(jnp.float32), keys.astype(jnp.float32))
    row_pos = lax.broadcasted_iota(jnp.int32, (count, count + window), 0)
    col_pos = lax.broadcasted_iota(jnp.int32, (count, count + window), 1)
    valid = (col_pos >= row_pos) & (col_pos <= row_pos + window) & (col_pos + start >= window)
    scores = jnp.where(valid[None], scores, -1e+30)
    highest = lax.optimization_barrier(jnp.max(scores, axis=2, keepdims=True))
    weights = jnp.exp(scores - highest)
    probs = (weights / lax.optimization_barrier(jnp.sum(weights, axis=2, keepdims=True))).astype(jnp.bfloat16)
    return jnp.einsum('sqk,skd->sqd', probs.astype(jnp.float32), values.astype(jnp.float32))

def combine(attended_output, fast, gain):
    normed = fast * lax.rsqrt(lax.optimization_barrier(jnp.mean(fast * fast, axis=-1, keepdims=True)) + 1e-05) * gain
    return (attended_output + normed).astype(jnp.bfloat16)

def reference(sequence_activity, lookup_mapping_tensor, stepsize_mapping_matrix, logit_sharpness, adapter_gain_vector, starting_inner_left_matrix, starting_inner_right_matrix, final_mixing_matrix):
    flattened = sequence_activity.reshape(SEQS * L, D)

    def one_branch_apply(packed):
        proj_head, rate_head, scale, gain, start_in, start_out = packed
        projected = jnp.dot(flattened, proj_head, preferred_element_type=jnp.float32)
        rate_col = jnp.dot(flattened, rate_head[:, None], preferred_element_type=jnp.float32)
        query_rows, keys, values, weighted = prepare(projected, rate_col, SEQS)
        padding = jnp.zeros((SEQS, WIN, DH), jnp.bfloat16)
        key_pad = jnp.concatenate([padding, keys], axis=1)
        value_pad = jnp.concatenate([padding, values], axis=1)
        state_in = jnp.broadcast_to(start_in, (SEQS,) + start_in.shape)
        state_out = jnp.broadcast_to(start_out, (SEQS,) + start_out.shape)
        pieces = []
        for block in range(N_SEQ):
            lower = block * GROUP
            attended_output = attend_window(query_rows[:, lower:lower + GROUP], key_pad[:, lower:lower + GROUP + WIN], value_pad[:, lower:lower + GROUP + WIN], scale, lower)
            state_in, state_out, fast = jax.vmap(fast_group)(state_in, state_out, keys[:, lower:lower + GROUP], weighted[:, lower:lower + GROUP], query_rows[:, lower:lower + GROUP])
            pieces.append(combine(attended_output, fast, gain))
        return jnp.concatenate(pieces, axis=1)
    number_of_branches = lax.map(one_branch_apply, (jnp.moveaxis(lookup_mapping_tensor, 1, 0), stepsize_mapping_matrix.T, logit_sharpness, adapter_gain_vector, starting_inner_left_matrix, starting_inner_right_matrix))
    stacked = jnp.transpose(number_of_branches, (1, 2, 0, 3)).reshape(SEQS * L, HEADS * DH)
    mixed = jnp.dot(stacked, final_mixing_matrix.reshape(HEADS * DH, D), preferred_element_type=jnp.float32)
    return mixed.astype(jnp.bfloat16).reshape(SEQS, L, D)
```

```python
import functools

import jax
import jax.numpy as jnp
from jax import lax
from jax.experimental import pallas as pl
from jax.experimental.pallas import tpu as pltpu
from jax.sharding import PartitionSpec as P

WIN = 2048
NS_STEPS = 3
UPDATE_RATE = 0.3
PAD_ROWS = 16


NT = (((1,), (1,)), ((), ()))
ANY = pl.BlockSpec(memory_space=pl.ANY)
VMEM = pl.BlockSpec(memory_space=pltpu.VMEM)
SMEM = pl.BlockSpec(memory_space=pltpu.SMEM)


def dot(a, b):
    return jnp.dot(a, b, preferred_element_type=jnp.float32)


def dot_nt(a, b):
    return lax.dot_general(a, b, NT, preferred_element_type=jnp.float32)


def chip_shift(block, chips):
    count = lax.axis_size("head")
    return lax.ppermute(block, "head", [(i, (i + 2 * chips) % count) for i in range(count)])


def core_swap(block):
    count = lax.axis_size("head")
    return lax.ppermute(block, "head", [(i, i ^ 1) for i in range(count)])


def later(block, distance):
    count = lax.axis_size("seq")
    return lax.ppermute(block, "seq", [(i, i + distance) for i in range(count - distance)])


def after(block, *others):
    return lax.optimization_barrier((block,) + others)[0]


def chip_offsets(chips):
    result = [0]
    for step in range(1, chips // 2 + 1):
        result.append(-step)
        if step < chips - step:
            result.append(step)
    return result


def ring_gather(block, chips):
    result = [block]
    up = down = block
    for step in range(1, chips // 2 + 1):
        up = chip_shift(up, 1)
        result.append(up)
        if step < chips - step:
            down = chip_shift(down, -1)
            result.append(down)
    return result


def project_kernel(blocks, idx_ref, *refs):
    x_refs = refs[:blocks]
    w_ref, step_ref, q_ref, kv_ref, x_full, sems = refs[blocks:]
    rows, width = x_refs[0].shape
    head = w_ref.shape[1] // 3
    copies = []
    for b in range(blocks):
        where = pl.ds(pl.multiple_of(idx_ref[b] * width, width), width)
        copies.append(pltpu.make_async_copy(x_refs[b], x_full.at[:, where], sems.at[b]))
        copies[-1].start()
    for copy in copies:
        copy.wait()
    x = x_full[...]
    q = dot(x, w_ref[:, :head])
    q_ref[...] = (q * lax.rsqrt(jnp.sum(q * q, axis=1, keepdims=True) + 1e-06)).astype(q_ref.dtype)
    k = dot(x, w_ref[:, head : 2 * head])
    kn = k * lax.rsqrt(jnp.sum(k * k, axis=1, keepdims=True) + 1e-06)
    kv_ref[:rows, :head] = kn.astype(kv_ref.dtype)
    kv_ref[:rows, head:] = dot(x, w_ref[:, 2 * head :]).astype(kv_ref.dtype)
    rate = dot_nt(step_ref[...], x)
    rate = jnp.concatenate([rate] * (PAD_ROWS // rate.shape[0]), axis=0)
    soft = jnp.maximum(rate, 0.0) + jnp.log1p(jnp.exp(-jnp.abs(rate)))
    kv_ref[rows:, :] = soft.astype(kv_ref.dtype)


def project(idx, pieces, weights, step_rows):
    rows, width = pieces[0].shape
    head = weights.shape[1] // 3
    blocks = len(pieces)
    return pl.pallas_call(
        functools.partial(project_kernel, blocks),
        out_shape=(
            jax.ShapeDtypeStruct((rows, head), jnp.bfloat16),
            jax.ShapeDtypeStruct((rows + PAD_ROWS, 2 * head), jnp.bfloat16),
        ),
        in_specs=[SMEM] + [ANY] * blocks + [VMEM, VMEM],
        out_specs=(VMEM, VMEM),
        scratch_shapes=[
            pltpu.VMEM((rows, blocks * width), jnp.bfloat16),
            pltpu.SemaphoreType.DMA((blocks,)),
        ],
        compiler_params=pltpu.CompilerParams(vmem_limit_bytes=32 << 20),
        cost_estimate=pl.CostEstimate(
            flops=2 * rows * blocks * width * 3 * head,
            bytes_accessed=2 * (blocks * width * (rows + 3 * head)),
            transcendentals=0,
        ),
        name="project",
    )(idx, *pieces, weights, step_rows)


def ortho(update):
    narrow = update.astype(jnp.bfloat16)
    gram = dot_nt(narrow, narrow)
    scale = lax.rsqrt(jnp.sum(update * update) + 1e-06)
    current = update * scale
    gram = gram * (scale * scale)
    for sweep in range(NS_STEPS):
        narrow = current.astype(jnp.bfloat16)
        if sweep:
            gram = dot_nt(narrow, narrow)
        current = 1.5 * current - 0.5 * dot(gram.astype(jnp.bfloat16), narrow)
    return current


def sigmoid(x):
    return 0.5 * jnp.tanh(0.5 * x) + 0.5


def block_kernel(count, reach, scal_ref, sharp_ref, q_ref, gain_ref, a0_ref, b0_ref, *refs):
    kv_refs = refs[:count]
    out_ref, kv_s, a_s, b_s, acc_s, m_s, l_s, sems = refs[count:]
    rows, head = q_ref.shape
    hidden = a0_ref.shape[1]
    place = scal_ref[0]
    sharp = sharp_ref[0]

    def fetch(slot, source):
        return pltpu.make_async_copy(source, kv_s.at[slot], sems.at[slot])

    for distance in range(count):

        @pl.when(place >= distance)
        def _():
            fetch(count - 1 - distance, kv_refs[distance]).start()

    a_s[...] = a0_ref[...]
    b_s[...] = b0_ref[...]
    m_s[...] = jnp.full(m_s.shape, -1e30, jnp.float32)
    l_s[...] = jnp.zeros(l_s.shape, jnp.float32)
    acc_s[...] = jnp.zeros(acc_s.shape, jnp.float32)

    def attend(distance, keys, values):
        scores = sharp * dot_nt(q_ref[...], keys)
        row = lax.broadcasted_iota(jnp.int32, scores.shape, 0)
        col = lax.broadcasted_iota(jnp.int32, scores.shape, 1)
        back = row - col + distance * rows
        scores = jnp.where((back >= 0) & (back <= WIN), scores, -1e30)
        old = m_s[...]
        new = jnp.maximum(old, jnp.max(scores, axis=1, keepdims=True))
        weights = jnp.exp(scores - new)
        shrink = jnp.exp(old - new)
        m_s[...] = new
        l_s[...] = l_s[...] * shrink + jnp.sum(weights, axis=1, keepdims=True)
        acc_s[...] = acc_s[...] * shrink + dot(weights.astype(jnp.bfloat16), values)

    def turn(slot, carry):
        fetch(slot, kv_refs[0]).wait()
        distance = count - 1 - slot
        keys = kv_s[slot, :rows, :head]
        values = kv_s[slot, :rows, head:]
        soft = kv_s[slot, rows:, :].astype(jnp.float32)[:8]
        soft = jnp.concatenate([soft] * 16, axis=0).T
        soft = jnp.concatenate([soft] * (hidden // 128), axis=1)
        left = a_s[...]
        right = b_s[...]
        pre = dot(keys, left.astype(jnp.bfloat16))
        gating = sigmoid(pre)
        act = pre * gating
        grad_out = dot(values.T, (act * soft).astype(jnp.bfloat16))
        backward = dot(values, right.astype(jnp.bfloat16)) * soft
        slopes = (backward * gating * (1.0 + pre - act)).astype(jnp.bfloat16)
        grad_in = dot(keys.T, slopes)
        a_s[...] = left + UPDATE_RATE * ortho(grad_in)
        b_s[...] = right + UPDATE_RATE * ortho(grad_out)
        if count - 1 <= reach:
            attend(distance, keys, values)
        else:
            pl.when(distance <= reach)(lambda: attend(distance, keys, values))
        return carry

    lax.fori_loop(count - 1 - place, count, turn, 0)
    pre = dot(q_ref[...], a_s[...].astype(jnp.bfloat16))
    act = (pre * sigmoid(pre)).astype(jnp.bfloat16)
    fast = dot_nt(act, b_s[...].astype(jnp.bfloat16))
    normed = fast * lax.rsqrt(jnp.mean(fast * fast, axis=1, keepdims=True) + 1e-05) * gain_ref[...]
    out_ref[...] = (acc_s[...] / l_s[...] + normed).astype(out_ref.dtype)


def run_blocks(place, sharp, query, gain, start_in, start_out_t, kvs, reach):
    rows, head = query.shape
    hidden = start_in.shape[1]
    count = len(kvs)
    return pl.pallas_call(
        functools.partial(block_kernel, count, reach),
        out_shape=jax.ShapeDtypeStruct((rows, head), jnp.bfloat16),
        in_specs=[SMEM, SMEM, VMEM, VMEM, VMEM, VMEM] + [ANY] * count,
        out_specs=VMEM,
        scratch_shapes=[
            pltpu.VMEM((count,) + kvs[0].shape, jnp.bfloat16),
            pltpu.VMEM((head, hidden), jnp.float32),
            pltpu.VMEM((head, hidden), jnp.float32),
            pltpu.VMEM((rows, head), jnp.float32),
            pltpu.VMEM((rows, 1), jnp.float32),
            pltpu.VMEM((rows, 1), jnp.float32),
            pltpu.SemaphoreType.DMA((count,)),
        ],
        compiler_params=pltpu.CompilerParams(vmem_limit_bytes=32 << 20),
        cost_estimate=pl.CostEstimate(
            flops=count * 16 * rows * head * hidden, bytes_accessed=4 << 20, transcendentals=0
        ),
        name="blocks",
    )(place, sharp, query, gain, start_in, start_out_t, *kvs)


def mix_kernel(blocks, parts, place_ref, *refs):
    o_refs = refs[:blocks]
    w_refs = refs[blocks : blocks + parts]
    out_ref, o_full, w_full, sems = refs[blocks + parts :]
    head = o_refs[0].shape[1]
    share = w_refs[0].shape[1]
    copies = []
    for part in range(parts):
        where = pl.ds(pl.multiple_of((place_ref[0] ^ part) * share, share), share)
        copies.append(pltpu.make_async_copy(w_refs[part], w_full.at[:, where, :], sems.at[part]))
    for b in range(blocks):
        where = pl.ds(b * head, head)
        copies.append(pltpu.make_async_copy(o_refs[b], o_full.at[:, where], sems.at[parts + b]))
    for copy in copies:
        copy.start()
    for copy in copies:
        copy.wait()
    w = w_full[...].reshape(blocks * head, w_full.shape[2])
    out_ref[...] = dot(o_full[...], w).astype(out_ref.dtype)


def mix(place, outs, columns):
    rows, head = outs[0].shape
    blocks, share, width = columns[0].shape
    parts = len(columns)
    return pl.pallas_call(
        functools.partial(mix_kernel, blocks, parts),
        out_shape=jax.ShapeDtypeStruct((rows, width), jnp.bfloat16),
        in_specs=[SMEM] + [ANY] * (blocks + parts),
        out_specs=VMEM,
        scratch_shapes=[
            pltpu.VMEM((rows, blocks * head), jnp.bfloat16),
            pltpu.VMEM((blocks, head, width), jnp.bfloat16),
            pltpu.SemaphoreType.DMA((blocks + parts,)),
        ],
        compiler_params=pltpu.CompilerParams(vmem_limit_bytes=32 << 20),
        cost_estimate=pl.CostEstimate(
            flops=2 * rows * blocks * head * width, bytes_accessed=4 << 20, transcendentals=0
        ),
        name="mix",
    )(place, *outs, *columns)


def gather_columns(mixing, chips, core, chip, place, anchor):
    head, total = mixing.shape
    count = lax.axis_size("seq")
    share = head // count
    width = total // (2 * chips)
    rows = lax.dynamic_slice_in_dim(mixing, place * share, share, 0)
    rows = rows.reshape(share, chips, 2, width)
    mine = lax.dynamic_index_in_dim(rows, core, 2, keepdims=False)
    other = lax.dynamic_index_in_dim(rows, 1 - core, 2, keepdims=False)
    pair = jnp.stack([mine, core_swap(other)])
    pair = after(pair, anchor)

    def toward(offset):
        return lax.dynamic_index_in_dim(pair, (chip + offset) % chips, 2, keepdims=False)

    pieces = []
    for offset in chip_offsets(chips):
        piece = toward(-offset)
        pieces.append(chip_shift(piece, -offset) if offset else piece)
    held = jnp.concatenate(pieces, axis=0)[None]
    step = 1
    while step < count:
        got = lax.ppermute(held, "seq", [(i, i ^ step) for i in range(count)])
        held = jnp.concatenate([held, got], axis=0)
        step *= 2
    return [held[i] for i in range(count)]


def body(activity, lookup, stepsize, sharpness, gain, start_left, start_right, mixing):
    seqs, rows, width = activity.shape
    weights = lookup.reshape(lookup.shape[0], lookup.shape[2])
    devices = lax.axis_size("head")
    chips = devices // 2
    count = lax.axis_size("seq")
    me = lax.axis_index("head")
    chip, core = me // 2, me % 2
    place = lax.axis_index("seq")
    place_arr = place.astype(jnp.int32).reshape(1)
    offsets = chip_offsets(chips)
    idx = []
    for offset in offsets:
        there = (chip + offset) % chips * 2
        idx += [there + core, there + 1 - core]
    idx = jnp.stack(idx).astype(jnp.int32)
    step_rows = jnp.broadcast_to(stepsize.reshape(1, -1), (8, stepsize.shape[0]))
    start_out_t = start_right[0].T
    reach = WIN // rows

    def gathered(block):
        pieces = []
        for piece in ring_gather(block, chips):
            pieces += [piece, core_swap(piece)]
        return pieces

    outs = []
    anchor = None
    projected = []
    for seq in range(seqs):
        block = activity[seq]
        if anchor is not None:
            block = after(block, anchor)
        pieces = gathered(block)
        anchor = pieces[-2]
        projected.append(project(idx, pieces, weights, step_rows))
    columns = gather_columns(mixing[0], chips, core, chip, place, anchor)
    for seq in range(seqs):
        query, kv = projected[seq]
        kvs = [kv] + [later(kv, distance) for distance in range(1, count)]
        outs.append(
            run_blocks(
                place_arr, sharpness, query, gain, start_left[0], start_out_t, kvs, reach
            )
        )
    results = [mix(place_arr, gathered(out), columns) for out in outs]
    return jnp.stack(results)


def solution(mesh):
    in_specs = (
        P(None, "seq", "head"),
        P(None, "head", None),
        P(None, "head"),
        P("head"),
        P("head", None),
        P("head", None, None),
        P("head", None, None),
        P("head", None, None),
    )
    out_specs = P(None, "seq", "head")
    return jax.shard_map(body, mesh=mesh, in_specs=in_specs, out_specs=out_specs, check_vma=False)
```
